512 devices in a mesh: tm: 64 (over y, z), state: 8 (over x, core).
Axes of the slice: x: 4, y: 4, z: 16, core: 2. Of those that a mesh axis runs over, the one named last changes fastest.
Arguments:
- obs: int32 [512], P('tm'), may hold values from 0 to 255
- emit_logits: float32 [256, 2048], P(None, 'state'), may hold values from -0.6 to 0.6
- trans_logits: float32 [16, 3, 128, 128], P('state'), may hold values from -5 to 17
- band_cols: int32 [16, 3], replicated, may hold values from 0 to 15, as said below
- init_logits: float32 [2048], replicated, may hold values from -6 to 6
Outputs:
- posterior: float32 [64, 2048], P('tm', 'state')
The draws below stay inside these ranges and needn't reach their ends.
Inputs may be any that keep to these rules, and one draw needn't show every extreme that they name: Row r of band_cols names 3 different block columns, the first of them r itself.
All inputs are finite; a program needn't handle non-finite values.
Results may differ from the reference program's by a relative error of at most 0.0006.
The reference program's roundings to bfloat16 on the way (of `blocks`, `scaled` and `weights`) count: a program that leaves them out, or rounds other values in their place, can miss the bound.
Values may be sent and summed in bfloat16 or wider, within the bound.
A program may use at most 64 MiB of HBM per device.

```python
import jax
import jax.numpy as jnp
from jax import lax

S = 2048
BLK = 128
K = 3
V = 256
L = 8
SEQS = 1
NB = 16
GROUPS = 64
TSTEPS = 512
N_TM = 64


def draw_band_cols(key, part):
    nblock = S // BLK

    def one_row(row_index):
        offsets = jax.random.permutation(jax.random.fold_in(key, row_index), nblock - 1)[:K - 1] + 1
        offsets = jnp.concatenate([jnp.zeros((1,), jnp.int32), offsets.astype(jnp.int32)])
        return (row_index + offsets) % nblock
    return jax.vmap(one_row)(jnp.arange(nblock, dtype=jnp.int32)).astype(jnp.int32)


def draw_trans_logits(key, part):
    noise_key = jax.random.fold_in(key, 11)
    boost_key = jax.random.fold_in(key, 23)
    noise = jnp.clip(jax.random.normal(noise_key, (NB, K, BLK, BLK), jnp.float32), -5.0, 5.0)
    boost = jax.random.uniform(boost_key, (NB, BLK), jnp.float32, 10.0, 17.0)
    own_block = jnp.arange(K)[:, None, None] == 0
    diagonal = jnp.arange(BLK)[None, :, None] == jnp.arange(BLK)[None, None, :]
    marked = (own_block & diagonal).astype(jnp.float32)[None]
    return (noise * (1.0 - marked) + marked * boost[:, None, :, None]).astype(jnp.float32)


def set_ends(result, own_key, least, largest):
    shape = result.shape
    spot = [jax.random.randint(jax.random.fold_in(own_key, axis), (), 0, shape[axis]) for axis in range(len(shape))]
    result = result.at[tuple(spot)].set(least)
    longest = shape.index(max(shape))
    spot[longest] = (spot[longest] + 1) % shape[longest]
    return result.at[tuple(spot)].set(largest)


def shard_levels(key, dims, split, least, top_value):
    def one(dim, shards_of):
        steps = jax.random.uniform(jax.random.fold_in(jax.random.fold_in(key, 6), dim), (shards_of,), jnp.float32, least / len(split), top_value / len(split))
        return jnp.repeat(jnp.exp(steps), dims[dim] // shards_of).reshape((-1,) + (1,) * (len(dims) - dim - 1))

    gain = one(*split[0])
    for cut in split[1:]:
        gain = gain * one(*cut)
    return gain


def normal_values(stream_key, dims, width, limit, pieces=(), kind=jnp.bfloat16):
    drawn = width * jax.random.normal(stream_key, dims, jnp.float32)
    if pieces:
        drawn = drawn * shard_levels(stream_key, dims, pieces, -0.22, 0.18)
    return jnp.clip(drawn, -limit, limit).astype(kind)


def setup_inputs(seed: int = 0) -> dict:
    streams_of = jax.random.split(jax.random.key(seed), 6)
    obs = set_ends(jax.random.randint(streams_of[0], (TSTEPS,), 0, V), jax.random.fold_in(streams_of[0], 1), 0, V - 1).astype(jnp.int32)
    emit_logits = normal_values(streams_of[1], (V, S), 0.1, 0.6, ((1, 8),), jnp.float32)
    trans_logits = draw_trans_logits(jax.random.fold_in(streams_of[5], 71), 0)
    band_cols = draw_band_cols(jax.random.fold_in(streams_of[5], 71), 0)
    init_logits = normal_values(streams_of[4], (S,), 1.5, 6.0, (), jnp.float32)
    return {"obs": obs, "emit_logits": emit_logits, "trans_logits": trans_logits, "band_cols": band_cols, "init_logits": init_logits}


SMOOTH = 0.001


def form_group(emit_group, blocks, band_cols):
    matrix = jnp.eye(S, dtype=jnp.float32)
    col_scale = jnp.zeros((S,), jnp.float32)
    for moment in range(L - 1, -1, -1):
        scaled = (jnp.exp(emit_group[moment])[:, None] * matrix).astype(jnp.bfloat16)
        picked = scaled.reshape(NB, BLK, S)[band_cols]
        product = jnp.einsum("rkij,rkjs->ris", blocks.astype(jnp.float32), picked.astype(jnp.float32), precision=lax.Precision.HIGHEST).reshape(S, S)
        matrix = product + (SMOOTH / S) * jnp.sum(scaled.astype(jnp.float32), axis=0)[None, :]
        col_peak = jnp.max(matrix, axis=0)
        matrix = matrix / col_peak[None, :]
        col_scale = col_scale + jnp.log(col_peak)
    return jnp.log(matrix) + col_scale[None, :]


def pair_product(left_log, right_log):
    row_peak = jnp.max(right_log, axis=1)
    left_peak = jnp.max(left_log + row_peak[None, :], axis=1)
    weights = jnp.exp(left_log + row_peak[None, :] - left_peak[:, None]).astype(jnp.bfloat16)
    right_exp = jnp.exp(right_log - row_peak[:, None]).astype(jnp.bfloat16)
    return left_peak[:, None] + jnp.log(jnp.dot(weights, right_exp, preferred_element_type=jnp.float32))


def apply_vector(vector, matrix):
    return jax.nn.logsumexp(vector[:, None] + matrix, axis=0)


def reference(obs, emit_logits, trans_logits, band_cols, init_logits):
    blocks = ((1.0 - SMOOTH) * jax.nn.softmax(trans_logits, axis=(1, 3))).astype(jnp.bfloat16)
    log_emit = jax.nn.log_softmax(emit_logits, axis=0)
    emissions = log_emit[obs].reshape(N_TM, L, S)
    prior_log = jax.nn.log_softmax(init_logits)
    outputs = []
    for sequence in range(SEQS):
        first_group = sequence * GROUPS
        first_matrix = form_group(emissions[first_group], blocks, band_cols)
        alpha_first = apply_vector(prior_log, first_matrix)
        second_matrix = form_group(emissions[first_group + 1], blocks, band_cols)
        alpha_second = apply_vector(prior_log, pair_product(first_matrix, second_matrix))

        def advance(state_carry, emit_group):
            previous, older_alpha, newer_alpha = state_carry
            current = form_group(emit_group, blocks, band_cols)
            fresh_alpha = apply_vector(older_alpha, pair_product(previous, current))
            return (current, newer_alpha, fresh_alpha), fresh_alpha

        _, remaining = lax.scan(advance, (second_matrix, alpha_first, alpha_second), emissions[first_group + 2:first_group + GROUPS])
        outputs.append(jnp.concatenate([alpha_first[None], alpha_second[None], remaining], axis=0))
    alphas = jnp.concatenate(outputs, axis=0)
    return alphas - jax.nn.logsumexp(alphas, axis=1, keepdims=True)
```

```python
import functools
import math

import jax
import jax.numpy as jnp
from jax import lax
from jax.experimental import pallas as pl
from jax.experimental.pallas import tpu as pltpu
from jax.sharding import PartitionSpec as P

SMOOTH = 0.001
MESH = pl.DeviceIdType.MESH
RISES = (5, 11, 20, 32, 46)
SPAN_MAX = 1 + len(RISES)


def span_of(group):
    span = jnp.int32(1)
    for rise in RISES:
        span = span + (group >= rise).astype(jnp.int32)
    return span


def inverse_of(value):
    def halves(x):
        scaled = x * 4097.0
        high = scaled - (scaled - x)
        return high, x - high

    quotient = 1.0 / value
    product = value * quotient
    value_high, value_low = halves(value)
    quotient_high, quotient_low = halves(quotient)
    excess = value_high * quotient_high - product
    excess = excess + value_high * quotient_low + value_low * quotient_high + value_low * quotient_low
    return quotient + quotient * ((1.0 - product) - excess)


def gather_kernel(groups, peers, obs_ref, trans_ref, emit_ref, blocks_ref, emis_ref,
                  obs_all, obs_send, obs_recv, blk_send, blk_recv, em_send, em_recv):
    group = lax.axis_index("tm")
    me = lax.axis_index("state")
    core = me % 2
    chip = me // 2
    chips = peers // 2
    sibling = me + 1 - 2 * core
    own_rows = trans_ref.shape[0]
    steps = obs_ref.shape[0]

    barrier = pltpu.get_barrier_semaphore()
    for other in range(1, peers):
        pl.semaphore_signal(barrier, inc=1, device_id=(group, (me + other) % peers), device_id_type=MESH)
    for back in range(1, SPAN_MAX):
        for target in ((group + back) % groups, (group + groups - back) % groups):
            pl.semaphore_signal(barrier, inc=1, device_id=(target, me), device_id_type=MESH)

    for row in range(own_rows):
        tiles = [trans_ref[row, k] for k in range(trans_ref.shape[1])]
        top = jnp.max(functools.reduce(jnp.maximum, tiles), axis=1, keepdims=True)
        tiles = [jnp.exp(tile - top) for tile in tiles]
        width = tiles[0].shape[1]
        totals = []
        for tile in tiles:
            for shift in (16, 32, 64, 8, 4, 2, 1):
                tile = tile + pltpu.roll(tile, width - shift, 1)
            totals.append(tile)
        inverse = inverse_of(functools.reduce(jnp.add, totals)[:, :1])
        for k, tile in enumerate(tiles):
            blocks_ref[own_rows * me + row, :, k * width:(k + 1) * width] = (
                (1.0 - SMOOTH) * (tile * inverse)).astype(jnp.bfloat16)

    pl.semaphore_wait(barrier, peers - 1 + 2 * (SPAN_MAX - 1))

    def obs_copy(back):
        return pltpu.make_async_remote_copy(
            src_ref=obs_ref, dst_ref=obs_all.at[back], send_sem=obs_send.at[back], recv_sem=obs_recv.at[back],
            device_id=((group + back) % groups, me), device_id_type=MESH)

    def block_copy(owner, target, sem):
        rows = blocks_ref.at[pl.ds(own_rows * owner, own_rows)]
        return pltpu.make_async_remote_copy(
            src_ref=rows, dst_ref=rows, send_sem=blk_send.at[sem], recv_sem=blk_recv.at[owner],
            device_id=(group, target), device_id_type=MESH)

    def emis_copy(owner, target, sem):
        part = emis_ref.at[owner]
        return pltpu.make_async_remote_copy(
            src_ref=part, dst_ref=part, send_sem=em_send.at[sem], recv_sem=em_recv.at[owner],
            device_id=(group, target), device_id_type=MESH)

    obs_copies = [obs_copy(back) for back in range(1, SPAN_MAX)]
    for copy in obs_copies:
        copy.start()
    sent = []
    for away in (2, 1, 3)[:chips - 1]:
        sent.append(block_copy(me, 2 * ((chip + away) % chips) + core, away))
        sent[-1].start()
    sent.append(block_copy(me, sibling, 0))
    sent[-1].start()

    logits = emit_ref[...]
    weights = jnp.exp(logits - jnp.max(logits, axis=0, keepdims=True))
    table = weights / jnp.sum(weights, axis=0, keepdims=True)
    obs_all[0] = obs_ref[...]
    for copy in obs_copies:
        copy.wait()
    symbols = logits.shape[0]
    seen = obs_all[...].reshape(SPAN_MAX * steps, obs_ref.shape[1])
    lane = lax.broadcasted_iota(jnp.int32, seen.shape, 1)
    onehot = jnp.concatenate(
        [(seen == lane + first).astype(jnp.float32) for first in range(0, symbols, seen.shape[1])], axis=1)
    emis_ref[me] = jnp.dot(onehot, table, precision=lax.Precision.HIGHEST, preferred_element_type=jnp.float32)
    for other in range(1, peers):
        sent.append(emis_copy(me, (me + other) % peers, other))
        sent[-1].start()

    for away in (1, 3, 2)[:chips - 1]:
        owner = 2 * ((chip + chips - away) % chips) + core
        block_copy(owner, sibling, 0).wait_recv()
        sent.append(block_copy(owner, sibling, chips + away))
        sent[-1].start()
    for away in range(chips):
        block_copy(2 * ((chip + away) % chips) + 1 - core, sibling, 0).wait_recv()
    for other in range(1, peers):
        emis_copy((me + other) % peers, sibling, 0).wait_recv()
    for copy in sent:
        copy.wait_send()


def form_kernel(band_ref, blocks_ref, emis_ref, high_ref, low_ref, gain_ref, matrix, scaled):
    group = lax.axis_index("tm")
    me = lax.axis_index("state")
    block_rows, block, cols = matrix.shape
    filled = blocks_ref.shape[2] // block
    states = block_rows * block
    log_symbols = math.log(256.0)
    steps = 8
    row_id = lax.broadcasted_iota(jnp.int32, (block, cols), 0)
    col_id = lax.broadcasted_iota(jnp.int32, (block, cols), 1)
    for r in range(block_rows):
        matrix[r] = (row_id + r * block == col_id + me * cols).astype(jnp.float32)

    def step(index, carry):
        inverse, log_scale = carry
        tile = pl.ds(pl.multiple_of((index // steps) * steps, steps), steps)
        now = lax.broadcasted_iota(jnp.int32, (steps, cols), 0) == steps - 1 - index % steps
        col_sum = jnp.zeros((8, cols), jnp.float32)
        for r in range(block_rows):
            start = r * block
            if start % cols == 0:
                row = jnp.sum(jnp.where(now, emis_ref[start // cols, tile, :], 0.0), axis=0, keepdims=True)
            column = jnp.broadcast_to(row[:, start % cols:start % cols + block], (block, block)).T
            column = jnp.concatenate([column] * (cols // block), axis=1)
            part = (column * (matrix[r] * inverse)).astype(jnp.bfloat16)
            scaled[r] = part
            col_sum = col_sum + jnp.sum(part.astype(jnp.float32).reshape(block // 8, 8, cols), axis=0)
        smooth = (SMOOTH / states) * jnp.sum(col_sum, axis=0, keepdims=True)
        peak = jnp.zeros((8, cols), jnp.float32)
        for r in range(block_rows):
            picked = jnp.concatenate([scaled[band_ref[r, k]] for k in range(filled)], axis=0)
            product = jnp.dot(blocks_ref[r], picked, preferred_element_type=jnp.float32) + smooth
            matrix[r] = product
            peak = jnp.maximum(peak, jnp.max(product.reshape(block // 8, 8, cols), axis=0))
        peak = jnp.max(peak, axis=0, keepdims=True)
        return 1.0 / peak, log_scale + (jnp.log(peak) + log_symbols)

    inverse, log_scale = lax.fori_loop(
        0, steps * span_of(group), step, (jnp.ones((1, cols), jnp.float32), jnp.zeros((1, cols), jnp.float32)))
    gain_ref[...] = jnp.exp(log_scale)
    for r in range(block_rows):
        whole = matrix[r] * inverse
        high = whole.astype(jnp.bfloat16)
        high_ref[r] = high
        low_ref[r] = (whole - high.astype(jnp.float32)).astype(jnp.bfloat16)


def chain_kernel(groups, peers, init_ref, high_ref, low_ref, gain_ref, out_ref,
                 parts, peer_parts, mine, recv, send, peer_send, peer_recv):
    group = lax.axis_index("tm")
    me = lax.axis_index("state")
    source = group - span_of(group)
    has_source = source >= 0
    feeds = [
        jnp.logical_and(group + ahead < groups, span_of(group + ahead) == ahead)
        for ahead in range(1, SPAN_MAX + 1)
    ]

    barrier = pltpu.get_barrier_semaphore()
    expected = jnp.int32(peers - 1)
    for other in range(1, peers):
        pl.semaphore_signal(barrier, inc=1, device_id=(group, (me + other) % peers), device_id_type=MESH)

    @pl.when(has_source)
    def _():
        for peer in range(peers):
            pl.semaphore_signal(barrier, inc=1, device_id=(source, peer), device_id_type=MESH)

    expected = expected + peers * has_source.astype(jnp.int32)
    for ahead, fed in enumerate(feeds, 1):
        @pl.when(fed)
        def _():
            for peer in range(peers):
                pl.semaphore_signal(barrier, inc=1, device_id=(group + ahead, peer), device_id_type=MESH)

        expected = expected + peers * fed.astype(jnp.int32)

    def onward(ahead, slot, peer):
        return pltpu.make_async_remote_copy(
            src_ref=mine, dst_ref=parts.at[slot], send_sem=send.at[ahead, peer], recv_sem=recv.at[slot],
            device_id=(group + ahead, peer), device_id_type=MESH)

    def to_peer(slot, peer, sem):
        return pltpu.make_async_remote_copy(
            src_ref=mine, dst_ref=peer_parts.at[slot], send_sem=peer_send.at[sem], recv_sem=peer_recv.at[slot],
            device_id=(group, peer), device_id_type=MESH)

    @pl.when(jnp.logical_not(has_source))
    def _():
        parts[...] = jnp.exp(init_ref[...] - jnp.max(init_ref[...]))

    @pl.when(has_source)
    def _():
        for peer in range(peers):
            onward(0, peer, 0).wait_recv()

    width = parts.shape[2]
    first_row = lax.broadcasted_iota(jnp.int32, (16, width), 0) == 0
    by_high = jnp.zeros((16, width), jnp.float32)
    by_low = jnp.zeros((16, width), jnp.float32)
    total = jnp.zeros((1, width), jnp.float32)
    depth = high_ref.shape[1]
    for peer in range(peers):
        part = parts[peer]
        total = total + part
        spread = jnp.broadcast_to(part, (16, width))
        rest = spread - spread.astype(jnp.bfloat16).astype(jnp.float32)
        both = jnp.where(first_row, spread, rest).astype(jnp.bfloat16)
        rows = slice(peer * (width // depth), (peer + 1) * (width // depth))
        by_high += jnp.dot(both, high_ref[rows].reshape(width, width), preferred_element_type=jnp.float32)
        by_low += jnp.dot(both, low_ref[rows].reshape(width, width), preferred_element_type=jnp.float32)
    norm = gain_ref[...] / jnp.sum(total, axis=1, keepdims=True)
    fresh = (by_high[0:1] + by_high[1:2] + by_low[0:1]) * norm
    mine[...] = fresh

    pl.semaphore_wait(barrier, expected)
    for ahead, fed in enumerate(feeds, 1):
        @pl.when(fed)
        def _():
            for peer in range(peers):
                onward(ahead, me, peer).start()

    for other in range(1, peers):
        to_peer(me, (me + other) % peers, other).start()
    whole = fresh
    for other in range(1, peers):
        slot = (me + other) % peers
        to_peer(slot, slot, other).wait_recv()
        whole = whole + peer_parts[slot]
    out_ref[...] = jnp.log(fresh) - jnp.log(jnp.sum(whole, axis=1, keepdims=True))
    for other in range(1, peers):
        to_peer(me, (me + other) % peers, other).wait_send()
    for ahead, fed in enumerate(feeds, 1):
        @pl.when(fed)
        def _():
            for peer in range(peers):
                onward(ahead, me, peer).wait_send()


def on_device(obs, emit_logits, trans_logits, band_cols, init_logits):
    peers = lax.axis_size("state")
    groups = lax.axis_size("tm")
    cols = emit_logits.shape[1]
    own_rows, filled, block, _ = trans_logits.shape
    block_rows = own_rows * peers
    steps = obs.shape[0]
    vmem = pl.BlockSpec(memory_space=pltpu.VMEM)
    dma = pltpu.SemaphoreType.DMA

    obs_wide = jnp.broadcast_to(obs[:, None], (steps, 128))
    blocks, emis = pl.pallas_call(
        functools.partial(gather_kernel, groups, peers),
        out_shape=(
            jax.ShapeDtypeStruct((block_rows, block, filled * block), jnp.bfloat16),
            jax.ShapeDtypeStruct((peers, SPAN_MAX * steps, cols), jnp.float32),
        ),
        in_specs=[vmem] * 3,
        out_specs=(vmem, vmem),
        scratch_shapes=[
            pltpu.VMEM((SPAN_MAX, steps, 128), jnp.int32),
            dma((SPAN_MAX,)), dma((SPAN_MAX,)),
            dma((peers,)), dma((peers,)),
            dma((peers,)), dma((peers,)),
        ],
        compiler_params=pltpu.CompilerParams(
            collective_id=0, has_side_effects=True, vmem_limit_bytes=32 * 2**20),
        name="gather",
    )(obs_wide, trans_logits, emit_logits)

    high, low, gain = pl.pallas_call(
        form_kernel,
        out_shape=(
            jax.ShapeDtypeStruct((block_rows, block, cols), jnp.bfloat16),
            jax.ShapeDtypeStruct((block_rows, block, cols), jnp.bfloat16),
            jax.ShapeDtypeStruct((1, cols), jnp.float32),
        ),
        in_specs=[pl.BlockSpec(memory_space=pltpu.SMEM), vmem, vmem],
        out_specs=(vmem, vmem, vmem),
        scratch_shapes=[
            pltpu.VMEM((block_rows, block, cols), jnp.float32),
            pltpu.VMEM((block_rows, block, cols), jnp.bfloat16),
        ],
        compiler_params=pltpu.CompilerParams(vmem_limit_bytes=40 * 2**20),
        name="form",
    )(band_cols, blocks, emis)

    return pl.pallas_call(
        functools.partial(chain_kernel, groups, peers),
        out_shape=jax.ShapeDtypeStruct((1, cols), jnp.float32),
        in_specs=[vmem] * 4,
        out_specs=vmem,
        scratch_shapes=[
            pltpu.VMEM((peers, 1, cols), jnp.float32),
            pltpu.VMEM((peers, 1, cols), jnp.float32),
            pltpu.VMEM((1, cols), jnp.float32),
            dma((peers,)), dma((SPAN_MAX + 1, peers)),
            dma((peers,)), dma((peers,)),
        ],
        compiler_params=pltpu.CompilerParams(
            collective_id=1, has_side_effects=True, vmem_limit_bytes=32 * 2**20),
        name="chain",
    )(init_logits.reshape(peers, 1, cols), high, low, gain)


def solution(mesh):
    return jax.shard_map(
        on_device,
        mesh=mesh,
        in_specs=(P("tm"), P(None, "state"), P("state", None, None, None), P(), P()),
        out_specs=P("tm", "state"),
        check_vma=False,
    )
```

```python
import functools
import math

import jax
import jax.numpy as jnp
from jax import lax
from jax.experimental import pallas as pl
from jax.experimental.pallas import tpu as pltpu
from jax.sharding import PartitionSpec as P

SMOOTH = 0.001
MESH = pl.DeviceIdType.MESH
DEEP = 16
RISES = (4, 13, 20, 50, 53, 57)
SPAN_MAX = 1 + len(RISES)


def span_of(group):
    span = jnp.int32(1)
    for rise in RISES:
        span = span + (group >= rise).astype(jnp.int32)
    return span


def group_at(place, groups):
    return place % DEEP * (groups // DEEP) + place // DEEP


def place_of(group, groups):
    high = groups // DEEP
    return group % high * DEEP + group // high


def when_all(*conditions):
    return pl.when(functools.reduce(jnp.logical_and, conditions))


def inverse_of(value):
    def halves(x):
        scaled = x * 4097.0
        high = scaled - (scaled - x)
        return high, x - high

    quotient = 1.0 / value
    product = value * quotient
    value_high, value_low = halves(value)
    quotient_high, quotient_low = halves(quotient)
    excess = value_high * quotient_high - product
    excess = excess + value_high * quotient_low + value_low * quotient_high + value_low * quotient_low
    return quotient + quotient * ((1.0 - product) - excess)


def gather_kernel(groups, peers, obs_ref, trans_hbm, emit_hbm, blocks_ref, emis_ref,
                  trans_ref, emit_ref, load, obs_all, obs_send, obs_recv, blk_send, blk_recv, em_send, em_recv):
    place = lax.axis_index("tm")
    group = group_at(place, groups)
    me = lax.axis_index("state")
    core = me % 2
    chip = me // 2
    chips = peers // 2
    sibling = me + 1 - 2 * core
    own_rows = trans_ref.shape[0]
    steps = obs_all.shape[1]
    loads = [pltpu.make_async_copy(trans_hbm, trans_ref, load.at[0]),
             pltpu.make_async_copy(emit_hbm, emit_ref, load.at[1])]
    for copy in loads:
        copy.start()

    def feeds(back):
        later = place + back
        used = jnp.logical_and(later < groups, span_of(later) > back)
        target = place_of(later, groups)
        return used, target, target == place

    def fed_by(back):
        used = jnp.logical_and(group >= back, span_of(group) > back)
        origin = group - back
        return used, origin, origin == place

    barrier = pltpu.get_barrier_semaphore()
    for other in range(1, peers):
        pl.semaphore_signal(barrier, inc=1, device_id=(place, (me + other) % peers), device_id_type=MESH)
    expected = jnp.int32(peers - 1)
    for back in range(SPAN_MAX):
        for side in (feeds, fed_by):
            used, partner, same = side(back)
            far = jnp.logical_and(used, jnp.logical_not(same))

            @pl.when(far)
            def _():
                pl.semaphore_signal(barrier, inc=1, device_id=(partner, me), device_id_type=MESH)

            expected = expected + far.astype(jnp.int32)

    loads[0].wait()
    for row in range(own_rows):
        tiles = [trans_ref[row, k] for k in range(trans_ref.shape[1])]
        top = jnp.max(functools.reduce(jnp.maximum, tiles), axis=1, keepdims=True)
        tiles = [jnp.exp(tile - top) for tile in tiles]
        width = tiles[0].shape[1]
        totals = []
        for tile in tiles:
            for shift in (16, 32, 64, 8, 4, 2, 1):
                tile = tile + pltpu.roll(tile, width - shift, 1)
            totals.append(tile)
        inverse = inverse_of(functools.reduce(jnp.add, totals)[:, :1])
        for k, tile in enumerate(tiles):
            blocks_ref[own_rows * me + row, :, k * width:(k + 1) * width] = (
                (1.0 - SMOOTH) * (tile * inverse)).astype(jnp.bfloat16)

    pl.semaphore_wait(barrier, expected)

    def obs_copy(back, target):
        return pltpu.make_async_remote_copy(
            src_ref=obs_ref, dst_ref=obs_all.at[back], send_sem=obs_send.at[back], recv_sem=obs_recv.at[back],
            device_id=(target, me), device_id_type=MESH)

    def block_copy(owner, target, sem):
        rows = blocks_ref.at[pl.ds(own_rows * owner, own_rows)]
        return pltpu.make_async_remote_copy(
            src_ref=rows, dst_ref=rows, send_sem=blk_send.at[sem], recv_sem=blk_recv.at[owner],
            device_id=(place, target), device_id_type=MESH)

    def emis_copy(owner, target, sem):
        part = emis_ref.at[owner]
        return pltpu.make_async_remote_copy(
            src_ref=part, dst_ref=part, send_sem=em_send.at[sem], recv_sem=em_recv.at[owner],
            device_id=(place, target), device_id_type=MESH)

    for back in range(SPAN_MAX):
        used, target, same = feeds(back)

        @when_all(used, jnp.logical_not(same))
        def _():
            obs_copy(back, target).start()

        @when_all(used, same)
        def _():
            obs_all[back] = obs_ref[...]

        @pl.when(jnp.logical_not(fed_by(back)[0]))
        def _():
            obs_all[back] = jnp.zeros(obs_ref.shape, obs_ref.dtype)

    sent = []
    for away in (2, 1, 3)[:chips - 1]:
        sent.append(block_copy(me, 2 * ((chip + away) % chips) + core, away))
        sent[-1].start()
    sent.append(block_copy(me, sibling, 0))
    sent[-1].start()

    loads[1].wait()
    logits = emit_ref[...]
    weights = jnp.exp(logits - jnp.max(logits, axis=0, keepdims=True))
    table = weights / jnp.sum(weights, axis=0, keepdims=True)
    for back in range(SPAN_MAX):
        used, origin, same = fed_by(back)

        @when_all(used, jnp.logical_not(same))
        def _():
            obs_copy(back, origin).wait_recv()

    symbols = logits.shape[0]
    seen = obs_all[...].reshape(SPAN_MAX * steps, obs_all.shape[2])
    lane = lax.broadcasted_iota(jnp.int32, seen.shape, 1)
    onehot = jnp.concatenate(
        [(seen == lane + first).astype(jnp.float32) for first in range(0, symbols, seen.shape[1])], axis=1)
    emis_ref[me] = jnp.dot(onehot, table, precision=lax.Precision.HIGHEST, preferred_element_type=jnp.float32)
    for other in range(1, peers):
        sent.append(emis_copy(me, (me + other) % peers, other))
        sent[-1].start()

    for away in (1, 3, 2)[:chips - 1]:
        owner = 2 * ((chip + chips - away) % chips) + core
        block_copy(owner, sibling, 0).wait_recv()
        sent.append(block_copy(owner, sibling, chips + away))
        sent[-1].start()
    for away in range(chips):
        block_copy(2 * ((chip + away) % chips) + 1 - core, sibling, 0).wait_recv()
    for other in range(1, peers):
        emis_copy((me + other) % peers, sibling, 0).wait_recv()
    for copy in sent:
        copy.wait_send()
    for back in range(SPAN_MAX):
        used, target, same = feeds(back)

        @when_all(used, jnp.logical_not(same))
        def _():
            obs_copy(back, target).wait_send()


def form_kernel(groups, band_hbm, blocks_ref, emis_ref, high_ref, low_ref, gain_ref, band_here, loaded, matrix, scaled):
    group = group_at(lax.axis_index("tm"), groups)
    me = lax.axis_index("state")
    block_rows, block, cols = matrix.shape
    filled = blocks_ref.shape[2] // block
    states = block_rows * block
    log_symbols = math.log(256.0)
    steps = 8
    row_id = lax.broadcasted_iota(jnp.int32, (block, cols), 0)
    col_id = lax.broadcasted_iota(jnp.int32, (block, cols), 1)
    load = pltpu.make_async_copy(band_hbm, band_here, loaded)
    load.start()
    for r in range(block_rows):
        matrix[r] = (row_id + r * block == col_id + me * cols).astype(jnp.float32)

    load.wait()

    def step(index, carry):
        inverse, log_scale = carry
        tile = pl.ds(pl.multiple_of((index // steps) * steps, steps), steps)
        now = lax.broadcasted_iota(jnp.int32, (steps, cols), 0) == steps - 1 - index % steps
        col_sum = jnp.zeros((8, cols), jnp.float32)
        for r in range(block_rows):
            start = r * block
            if start % cols == 0:
                row = jnp.sum(jnp.where(now, emis_ref[start // cols, tile, :], 0.0), axis=0, keepdims=True)
            column = jnp.broadcast_to(row[:, start % cols:start % cols + block], (block, block)).T
            column = jnp.concatenate([column] * (cols // block), axis=1)
            part = column * (matrix[r] * inverse)
            scaled[r] = part.astype(jnp.bfloat16)
            col_sum = col_sum + jnp.sum(part.reshape(block // 8, 8, cols), axis=0)
        smooth = (SMOOTH / states) * jnp.sum(col_sum, axis=0, keepdims=True)
        peak = jnp.zeros((8, cols), jnp.float32)
        for r in range(block_rows):
            picked = jnp.concatenate([scaled[band_here[k, r]] for k in range(filled)], axis=0)
            product = jnp.dot(blocks_ref[r], picked, preferred_element_type=jnp.float32) + smooth
            matrix[r] = product
            peak = jnp.maximum(peak, jnp.max(product.reshape(block // 8, 8, cols), axis=0))
        peak = jnp.max(peak, axis=0, keepdims=True)
        return 1.0 / peak, log_scale + (jnp.log(peak) + log_symbols)

    inverse, log_scale = lax.fori_loop(
        0, steps * span_of(group), step, (jnp.ones((1, cols), jnp.float32), jnp.zeros((1, cols), jnp.float32)))
    gain_ref[...] = jnp.exp(log_scale)
    for r in range(block_rows):
        whole = matrix[r] * inverse
        high = whole.astype(jnp.bfloat16)
        high_ref[r] = high
        low_ref[r] = (whole - high.astype(jnp.float32)).astype(jnp.bfloat16)


def chain_kernel(groups, peers, init_ref, high_ref, low_ref, gain_ref, out_ref,
                 parts, peer_parts, mine, recv, send, peer_send, peer_recv):
    place = lax.axis_index("tm")
    group = group_at(place, groups)
    me = lax.axis_index("state")
    source = group - span_of(group)
    has_source = source >= 0
    feeds = [
        jnp.logical_and(group + ahead < groups, span_of(group + ahead) == ahead)
        for ahead in range(1, SPAN_MAX + 1)
    ]

    barrier = pltpu.get_barrier_semaphore()
    expected = jnp.int32(peers - 1)
    for other in range(1, peers):
        pl.semaphore_signal(barrier, inc=1, device_id=(place, (me + other) % peers), device_id_type=MESH)

    @pl.when(has_source)
    def _():
        for peer in range(peers):
            pl.semaphore_signal(barrier, inc=1, device_id=(place_of(source, groups), peer), device_id_type=MESH)

    expected = expected + peers * has_source.astype(jnp.int32)
    for ahead, fed in enumerate(feeds, 1):
        @pl.when(fed)
        def _():
            for peer in range(peers):
                pl.semaphore_signal(barrier, inc=1, device_id=(place_of(group + ahead, groups), peer), device_id_type=MESH)

        expected = expected + peers * fed.astype(jnp.int32)

    def onward(ahead, slot, peer):
        return pltpu.make_async_remote_copy(
            src_ref=mine, dst_ref=parts.at[slot], send_sem=send.at[ahead, peer], recv_sem=recv.at[slot],
            device_id=(place_of(group + ahead, groups), peer), device_id_type=MESH)

    def to_peer(slot, peer, sem):
        return pltpu.make_async_remote_copy(
            src_ref=mine, dst_ref=peer_parts.at[slot], send_sem=peer_send.at[sem], recv_sem=peer_recv.at[slot],
            device_id=(place, peer), device_id_type=MESH)

    @pl.when(jnp.logical_not(has_source))
    def _():
        parts[...] = jnp.exp(init_ref[...] - jnp.max(init_ref[...]))

    @pl.when(has_source)
    def _():
        for peer in range(peers):
            onward(0, peer, 0).wait_recv()

    width = parts.shape[2]
    first_row = lax.broadcasted_iota(jnp.int32, (16, width), 0) == 0
    by_high = jnp.zeros((16, width), jnp.float32)
    by_low = jnp.zeros((16, width), jnp.float32)
    total = jnp.zeros((1, width), jnp.float32)
    depth = high_ref.shape[1]
    for peer in range(peers):
        part = parts[peer]
        total = total + part
        spread = jnp.broadcast_to(part, (16, width))
        rest = spread - spread.astype(jnp.bfloat16).astype(jnp.float32)
        both = jnp.where(first_row, spread, rest).astype(jnp.bfloat16)
        rows = slice(peer * (width // depth), (peer + 1) * (width // depth))
        by_high += jnp.dot(both, high_ref[rows].reshape(width, width), preferred_element_type=jnp.float32)
        by_low += jnp.dot(both, low_ref[rows].reshape(width, width), preferred_element_type=jnp.float32)
    norm = gain_ref[...] / jnp.sum(total, axis=1, keepdims=True)
    fresh = (by_high[0:1] + by_high[1:2] + by_low[0:1]) * norm
    mine[...] = fresh

    pl.semaphore_wait(barrier, expected)
    for ahead, fed in enumerate(feeds, 1):
        @pl.when(fed)
        def _():
            for turn in (4, 5, 2, 3, 6, 7, 1, 0):
                onward(ahead, me, (me - me % 2 + turn) % peers).start()

    for other in range(1, peers):
        to_peer(me, (me + other) % peers, other).start()
    whole = fresh
    for other in range(1, peers):
        slot = (me + other) % peers
        to_peer(slot, slot, other).wait_recv()
        whole = whole + peer_parts[slot]
    out_ref[...] = jnp.log(fresh) - jnp.log(jnp.sum(whole, axis=1, keepdims=True))
    for other in range(1, peers):
        to_peer(me, (me + other) % peers, other).wait_send()
    for ahead, fed in enumerate(feeds, 1):
        @pl.when(fed)
        def _():
            for peer in range(peers):
                onward(ahead, me, peer).wait_send()


def deliver_kernel(groups, found_ref, out_ref, send, recv):
    place = lax.axis_index("tm")
    me = lax.axis_index("state")
    target = group_at(place, groups)
    origin = place_of(place, groups)
    moves = target != place
    copy = pltpu.make_async_remote_copy(
        src_ref=found_ref, dst_ref=out_ref, send_sem=send, recv_sem=recv,
        device_id=(target, me), device_id_type=MESH)

    @pl.when(moves)
    def _():
        barrier = pltpu.get_barrier_semaphore()
        pl.semaphore_signal(barrier, inc=1, device_id=(origin, me), device_id_type=MESH)
        pl.semaphore_wait(barrier, 1)
        copy.start()
        copy.wait()

    @pl.when(jnp.logical_not(moves))
    def _():
        out_ref[...] = found_ref[...]


def on_device(obs, emit_logits, trans_logits, band_cols, init_logits):
    peers = lax.axis_size("state")
    groups = lax.axis_size("tm")
    cols = emit_logits.shape[1]
    own_rows, filled, block, _ = trans_logits.shape
    block_rows = own_rows * peers
    steps = obs.shape[0]
    vmem = pl.BlockSpec(memory_space=pltpu.VMEM)
    dma = pltpu.SemaphoreType.DMA

    hbm = pl.BlockSpec(memory_space=pltpu.HBM)
    obs_wide = jnp.broadcast_to(obs[:, None], (steps, 128))
    blocks, emis = pl.pallas_call(
        functools.partial(gather_kernel, groups, peers),
        out_shape=(
            jax.ShapeDtypeStruct((block_rows, block, filled * block), jnp.bfloat16),
            jax.ShapeDtypeStruct((peers, SPAN_MAX * steps, cols), jnp.float32),
        ),
        in_specs=[vmem, hbm, hbm],
        out_specs=(vmem, vmem),
        scratch_shapes=[
            pltpu.VMEM(trans_logits.shape, jnp.float32),
            pltpu.VMEM(emit_logits.shape, jnp.float32),
            dma((2,)),
            pltpu.VMEM((SPAN_MAX, steps, 128), jnp.int32),
            dma((SPAN_MAX,)), dma((SPAN_MAX,)),
            dma((peers,)), dma((peers,)),
            dma((peers,)), dma((peers,)),
        ],
        compiler_params=pltpu.CompilerParams(
            collective_id=0, has_side_effects=True, vmem_limit_bytes=32 * 2**20),
        name="gather",
    )(obs_wide, trans_logits, emit_logits)

    high, low, gain = pl.pallas_call(
        functools.partial(form_kernel, groups),
        out_shape=(
            jax.ShapeDtypeStruct((block_rows, block, cols), jnp.bfloat16),
            jax.ShapeDtypeStruct((block_rows, block, cols), jnp.bfloat16),
            jax.ShapeDtypeStruct((1, cols), jnp.float32),
        ),
        in_specs=[hbm, vmem, vmem],
        out_specs=(vmem, vmem, vmem),
        scratch_shapes=[
            pltpu.SMEM((filled, block_rows), jnp.int32),
            dma,
            pltpu.VMEM((block_rows, block, cols), jnp.float32),
            pltpu.VMEM((block_rows, block, cols), jnp.bfloat16),
        ],
        compiler_params=pltpu.CompilerParams(vmem_limit_bytes=40 * 2**20),
        name="form",
    )(band_cols.T, blocks, emis)

    found = pl.pallas_call(
        functools.partial(chain_kernel, groups, peers),
        out_shape=jax.ShapeDtypeStruct((1, cols), jnp.float32),
        in_specs=[vmem] * 4,
        out_specs=vmem,
        scratch_shapes=[
            pltpu.VMEM((peers, 1, cols), jnp.float32),
            pltpu.VMEM((peers, 1, cols), jnp.float32),
            pltpu.VMEM((1, cols), jnp.float32),
            dma((peers,)), dma((SPAN_MAX + 1, peers)),
            dma((peers,)), dma((peers,)),
        ],
        compiler_params=pltpu.CompilerParams(
            collective_id=1, has_side_effects=True, vmem_limit_bytes=32 * 2**20),
        name="chain",
    )(init_logits.reshape(peers, 1, cols), high, low, gain)

    return pl.pallas_call(
        functools.partial(deliver_kernel, groups),
        out_shape=jax.ShapeDtypeStruct((1, cols), jnp.float32),
        in_specs=[vmem],
        out_specs=vmem,
        scratch_shapes=[dma, dma],
        compiler_params=pltpu.CompilerParams(collective_id=2, has_side_effects=True, vmem_limit_bytes=2**20),
        name="deliver",
    )(found)


def solution(mesh):
    return jax.shard_map(
        on_device,
        mesh=mesh,
        in_specs=(P("tm"), P(None, "state"), P("state", None, None, None), P(), P()),
        out_specs=P("tm", "state"),
        check_vma=False,
    )
```

```python
import functools
import math

import jax
import jax.numpy as jnp
from jax import lax
from jax.experimental import pallas as pl
from jax.experimental.pallas import tpu as pltpu
from jax.sharding import PartitionSpec as P

SMOOTH = 0.001
MESH = pl.DeviceIdType.MESH
DEEP = 16
RISES = (5, 9, 17, 29, 33, 45)
SPAN_MAX = 1 + len(RISES)


def span_of(group):
    span = jnp.int32(1)
    for rise in RISES:
        span = span + (group >= rise).astype(jnp.int32)
    return span


def group_at(place, groups):
    high = groups // DEEP
    y, z = place // DEEP, place % DEEP
    return jnp.where(z < high, y * high + z, z * high + y)


def place_of(group, groups):
    high = groups // DEEP
    return jnp.where(
        group < high * high, group // high * DEEP + group % high, group % high * DEEP + group // high)


def when_all(*conditions):
    return pl.when(functools.reduce(jnp.logical_and, conditions))


def inverse_of(value):
    def halves(x):
        scaled = x * 4097.0
        high = scaled - (scaled - x)
        return high, x - high

    quotient = 1.0 / value
    product = value * quotient
    value_high, value_low = halves(value)
    quotient_high, quotient_low = halves(quotient)
    excess = value_high * quotient_high - product
    excess = excess + value_high * quotient_low + value_low * quotient_high + value_low * quotient_low
    return quotient + quotient * ((1.0 - product) - excess)


def gather_kernel(groups, peers, obs_ref, trans_hbm, emit_hbm, blocks_ref, emis_ref,
                  trans_ref, emit_ref, load, obs_all, obs_send, obs_recv, blk_send, blk_recv, em_send, em_recv):
    place = lax.axis_index("tm")
    group = group_at(place, groups)
    me = lax.axis_index("state")
    core = me % 2
    chip = me // 2
    chips = peers // 2
    sibling = me + 1 - 2 * core
    own_rows = trans_ref.shape[0]
    steps = obs_all.shape[1]
    loads = [pltpu.make_async_copy(trans_hbm, trans_ref, load.at[0]),
             pltpu.make_async_copy(emit_hbm, emit_ref, load.at[1])]
    for copy in loads:
        copy.start()

    def feeds(back):
        later = place + back
        used = jnp.logical_and(later < groups, span_of(later) > back)
        target = place_of(later, groups)
        return used, target, target == place

    def fed_by(back):
        used = jnp.logical_and(group >= back, span_of(group) > back)
        origin = group - back
        return used, origin, origin == place

    barrier = pltpu.get_barrier_semaphore()
    for other in range(1, peers):
        pl.semaphore_signal(barrier, inc=1, device_id=(place, (me + other) % peers), device_id_type=MESH)
    expected = jnp.int32(peers - 1)
    for back in range(SPAN_MAX):
        for side in (feeds, fed_by):
            used, partner, same = side(back)
            far = jnp.logical_and(used, jnp.logical_not(same))

            @pl.when(far)
            def _():
                pl.semaphore_signal(barrier, inc=1, device_id=(partner, me), device_id_type=MESH)

            expected = expected + far.astype(jnp.int32)

    loads[0].wait()
    for row in range(own_rows):
        tiles = [trans_ref[row, k] for k in range(trans_ref.shape[1])]
        top = jnp.max(functools.reduce(jnp.maximum, tiles), axis=1, keepdims=True)
        tiles = [jnp.exp(tile - top) for tile in tiles]
        width = tiles[0].shape[1]
        totals = []
        for tile in tiles:
            for shift in (16, 32, 64, 8, 4, 2, 1):
                tile = tile + pltpu.roll(tile, width - shift, 1)
            totals.append(tile)
        inverse = inverse_of(functools.reduce(jnp.add, totals)[:, :1])
        for k, tile in enumerate(tiles):
            blocks_ref[own_rows * me + row, :, k * width:(k + 1) * width] = (
                (1.0 - SMOOTH) * (tile * inverse)).astype(jnp.bfloat16)

    pl.semaphore_wait(barrier, expected)

    def obs_copy(back, target):
        return pltpu.make_async_remote_copy(
            src_ref=obs_ref, dst_ref=obs_all.at[back], send_sem=obs_send.at[back], recv_sem=obs_recv.at[back],
            device_id=(target, me), device_id_type=MESH)

    def block_copy(owner, row, target, sem):
        part = blocks_ref.at[own_rows * owner + row]
        return pltpu.make_async_remote_copy(
            src_ref=part, dst_ref=part, send_sem=blk_send.at[sem], recv_sem=blk_recv.at[own_rows * owner + row],
            device_id=(place, target), device_id_type=MESH)

    def emis_copy(owner, target, sem):
        part = emis_ref.at[owner]
        return pltpu.make_async_remote_copy(
            src_ref=part, dst_ref=part, send_sem=em_send.at[sem], recv_sem=em_recv.at[owner],
            device_id=(place, target), device_id_type=MESH)

    for back in range(SPAN_MAX):
        used, target, same = feeds(back)

        @when_all(used, jnp.logical_not(same))
        def _():
            obs_copy(back, target).start()

        @when_all(used, same)
        def _():
            obs_all[back] = obs_ref[...]

        @pl.when(jnp.logical_not(fed_by(back)[0]))
        def _():
            obs_all[back] = jnp.zeros(obs_ref.shape, obs_ref.dtype)

    sent = []

    def send_block(owner, row, target):
        sent.append(block_copy(owner, row, target, len(sent)))
        sent[-1].start()

    right = 2 * ((chip + 1) % chips) + core
    left = 2 * ((chip + chips - 1) % chips) + core
    across = 2 * ((chip + 2) % chips) + core
    for row, target in ((0, right), (1, left), (1, right), (0, left), (0, sibling), (1, sibling)):
        send_block(me, row, target)

    loads[1].wait()
    logits = emit_ref[...]
    weights = jnp.exp(logits - jnp.max(logits, axis=0, keepdims=True))
    table = weights / jnp.sum(weights, axis=0, keepdims=True)
    for back in range(SPAN_MAX):
        used, origin, same = fed_by(back)

        @when_all(used, jnp.logical_not(same))
        def _():
            obs_copy(back, origin).wait_recv()

    symbols = logits.shape[0]
    seen = obs_all[...].reshape(SPAN_MAX * steps, obs_all.shape[2])
    lane = lax.broadcasted_iota(jnp.int32, seen.shape, 1)
    onehot = jnp.concatenate(
        [(seen == lane + first).astype(jnp.float32) for first in range(0, symbols, seen.shape[1])], axis=1)
    emis_ref[me] = jnp.dot(onehot, table, precision=lax.Precision.HIGHEST, preferred_element_type=jnp.float32)
    for other in range(1, peers):
        emis_copy(me, (me + other) % peers, other).start()

    for owner, row, onward in ((left, 0, right), (right, 1, left), (left, 1, None), (right, 0, None),
                               (across, 0, None), (across, 1, None)):
        block_copy(owner, row, sibling, 0).wait_recv()
        if onward is not None:
            send_block(owner, row, onward)
        send_block(owner, row, sibling)
    for away in range(chips):
        for row in range(own_rows):
            block_copy(2 * ((chip + away) % chips) + 1 - core, row, sibling, 0).wait_recv()
    for other in range(1, peers):
        emis_copy((me + other) % peers, sibling, 0).wait_recv()
    for copy in sent:
        copy.wait_send()
    for other in range(1, peers):
        emis_copy(me, (me + other) % peers, other).wait_send()
    for back in range(SPAN_MAX):
        used, target, same = feeds(back)

        @when_all(used, jnp.logical_not(same))
        def _():
            obs_copy(back, target).wait_send()


def form_kernel(groups, band_hbm, blocks_ref, emis_ref, high_ref, low_ref, gain_ref, band_here, loaded, matrix, scaled, columns):
    group = group_at(lax.axis_index("tm"), groups)
    me = lax.axis_index("state")
    block_rows, block, cols = matrix.shape
    filled = blocks_ref.shape[2] // block
    states = block_rows * block
    log_symbols = math.log(256.0)
    steps = 8
    row_id = lax.broadcasted_iota(jnp.int32, (block, cols), 0)
    col_id = lax.broadcasted_iota(jnp.int32, (block, cols), 1)
    load = pltpu.make_async_copy(band_hbm, band_here, loaded)
    load.start()
    for r in range(block_rows):
        matrix[r] = (row_id + r * block == col_id + me * cols).astype(jnp.float32)

    def row_at(index, owner):
        tile = pl.ds(pl.multiple_of((index // steps) * steps, steps), steps)
        now = lax.broadcasted_iota(jnp.int32, (steps, cols), 0) == steps - 1 - index % steps
        return jnp.sum(jnp.where(now, emis_ref[owner, tile, :], 0.0), axis=0, keepdims=True)

    def set_column(r, row):
        start = r * block % cols
        columns[r] = jnp.broadcast_to(row[:, start:start + block], (block, block)).T

    for r in range(block_rows):
        set_column(r, row_at(0, r * block // cols))
    load.wait()

    def step(index, carry):
        inverse, log_scale = carry
        col_sum = jnp.zeros((8, cols), jnp.float32)
        for r in range(block_rows):
            column = jnp.concatenate([columns[r]] * (cols // block), axis=1)
            part = column * (matrix[r] * inverse)
            scaled[r] = part.astype(jnp.bfloat16)
            col_sum = col_sum + jnp.sum(part.reshape(block // 8, 8, cols), axis=0)
        smooth = (SMOOTH / states) * jnp.sum(col_sum, axis=0, keepdims=True)
        peak = jnp.zeros((8, cols), jnp.float32)
        following = jnp.minimum(index + 1, emis_ref.shape[1] - 1)
        for r in range(block_rows):
            picked = jnp.concatenate([scaled[band_here[k, r]] for k in range(filled)], axis=0)
            product = jnp.dot(blocks_ref[r], picked, preferred_element_type=jnp.float32) + smooth
            matrix[r] = product
            if r * block % cols == 0:
                row = row_at(following, r * block // cols)
            set_column(r, row)
            peak = jnp.maximum(peak, jnp.max(product.reshape(block // 8, 8, cols), axis=0))
        peak = jnp.max(peak, axis=0, keepdims=True)
        return 1.0 / peak, log_scale + (jnp.log(peak) + log_symbols)

    inverse, log_scale = lax.fori_loop(
        0, steps * span_of(group), step, (jnp.ones((1, cols), jnp.float32), jnp.zeros((1, cols), jnp.float32)))
    gain_ref[...] = jnp.exp(log_scale)
    for r in range(block_rows):
        whole = matrix[r] * inverse
        high = whole.astype(jnp.bfloat16)
        high_ref[r] = high
        low_ref[r] = (whole - high.astype(jnp.float32)).astype(jnp.bfloat16)


def chain_kernel(groups, peers, init_ref, high_ref, low_ref, gain_ref, out_ref,
                 parts, owned, mine, recv, send, own_send, own_recv, own_local, ready):
    place = lax.axis_index("tm")
    group = group_at(place, groups)
    me = lax.axis_index("state")
    source = group - span_of(group)
    has_source = source >= 0
    feeds = [
        jnp.logical_and(group + ahead < groups, span_of(group + ahead) == ahead)
        for ahead in range(1, SPAN_MAX + 1)
    ]
    origin = place_of(place, groups)
    at_home = group == place
    owned_later = place > group
    owned_earlier = place < group
    owner_first = group_at(group, groups) < group
    owner_later = group_at(group, groups) > group

    barrier = pltpu.get_barrier_semaphore()
    expected = jnp.int32(0)

    def greet(condition, target):
        @pl.when(condition)
        def _():
            for peer in range(peers):
                pl.semaphore_signal(barrier, inc=1, device_id=(target, peer), device_id_type=MESH)

    @pl.when(at_home)
    def _():
        for other in range(1, peers):
            pl.semaphore_signal(barrier, inc=1, device_id=(place, (me + other) % peers), device_id_type=MESH)

    greet(has_source, place_of(source, groups))
    expected = expected + (peers - 1) * at_home.astype(jnp.int32) + peers * has_source.astype(jnp.int32)
    for ahead, fed in enumerate(feeds, 1):
        greet(fed, place_of(group + ahead, groups))
        expected = expected + peers * fed.astype(jnp.int32)
    greet(owned_later, origin)
    greet(owner_later, group)
    expected = expected + peers * (owned_earlier.astype(jnp.int32) + owner_first.astype(jnp.int32))

    def onward(ahead, slot, peer):
        return pltpu.make_async_remote_copy(
            src_ref=mine, dst_ref=parts.at[slot], send_sem=send.at[ahead, peer], recv_sem=recv.at[slot],
            device_id=(place_of(group + ahead, groups), peer), device_id_type=MESH)

    def to_owner(slot, peer):
        return pltpu.make_async_remote_copy(
            src_ref=mine, dst_ref=owned.at[slot], send_sem=own_send.at[peer], recv_sem=own_recv.at[slot],
            device_id=(group, peer), device_id_type=MESH)

    pl.semaphore_wait(barrier, expected)

    @pl.when(owned_earlier)
    def _():
        for peer in range(peers):
            pl.semaphore_signal(ready, inc=1, device_id=(origin, peer), device_id_type=MESH)

    @pl.when(jnp.logical_not(has_source))
    def _():
        parts[...] = jnp.exp(init_ref[...] - jnp.max(init_ref[...]))

    @pl.when(has_source)
    def _():
        for peer in range(peers):
            onward(0, peer, 0).wait_recv()

    width = parts.shape[2]
    first_row = lax.broadcasted_iota(jnp.int32, (16, width), 0) == 0
    by_high = jnp.zeros((16, width), jnp.float32)
    by_low = jnp.zeros((16, width), jnp.float32)
    total = jnp.zeros((1, width), jnp.float32)
    depth = high_ref.shape[1]
    for peer in range(peers):
        part = parts[peer]
        total = total + part
        spread = jnp.broadcast_to(part, (16, width))
        rest = spread - spread.astype(jnp.bfloat16).astype(jnp.float32)
        both = jnp.where(first_row, spread, rest).astype(jnp.bfloat16)
        rows = slice(peer * (width // depth), (peer + 1) * (width // depth))
        by_high += jnp.dot(both, high_ref[rows].reshape(width, width), preferred_element_type=jnp.float32)
        by_low += jnp.dot(both, low_ref[rows].reshape(width, width), preferred_element_type=jnp.float32)
    norm = gain_ref[...] / jnp.sum(total, axis=1, keepdims=True)
    mine[...] = (by_high[0:1] + by_high[1:2] + by_low[0:1]) * norm

    for ahead, fed in enumerate(feeds, 1):
        @pl.when(fed)
        def _():
            for turn in (4, 5, 2, 3, 6, 7, 1, 0):
                onward(ahead, me, (me - me % 2 + turn) % peers).start()

    @pl.when(owner_later)
    def _():
        pl.semaphore_wait(ready, peers)

    @pl.when(at_home)
    def _():
        pltpu.make_async_copy(mine, owned.at[me], own_local).start()
        for other in range(1, peers):
            to_owner(me, (me + other) % peers).start()
        pltpu.make_async_copy(mine, owned.at[me], own_local).wait()
        for other in range(1, peers):
            to_owner((me + other) % peers, 0).wait_recv()
        for other in range(1, peers):
            to_owner(me, (me + other) % peers).wait_send()

    @pl.when(jnp.logical_not(at_home))
    def _():
        for peer in range(peers):
            to_owner(me, peer).start()
        for slot in range(peers):
            to_owner(slot, 0).wait_recv()
        for peer in range(peers):
            to_owner(me, peer).wait_send()

    whole = jnp.zeros((1, width), jnp.float32)
    for slot in range(peers):
        whole = whole + owned[slot]
    out_ref[...] = jnp.log(owned[me]) - jnp.log(jnp.sum(whole, axis=1, keepdims=True))
    for ahead, fed in enumerate(feeds, 1):
        @pl.when(fed)
        def _():
            for peer in range(peers):
                onward(ahead, me, peer).wait_send()


def on_device(obs, emit_logits, trans_logits, band_cols, init_logits):
    peers = lax.axis_size("state")
    groups = lax.axis_size("tm")
    cols = emit_logits.shape[1]
    own_rows, filled, block, _ = trans_logits.shape
    block_rows = own_rows * peers
    steps = obs.shape[0]
    vmem = pl.BlockSpec(memory_space=pltpu.VMEM)
    dma = pltpu.SemaphoreType.DMA

    hbm = pl.BlockSpec(memory_space=pltpu.HBM)
    obs_wide = jnp.broadcast_to(obs[:, None], (steps, 128))
    blocks, emis = pl.pallas_call(
        functools.partial(gather_kernel, groups, peers),
        out_shape=(
            jax.ShapeDtypeStruct((block_rows, block, filled * block), jnp.bfloat16),
            jax.ShapeDtypeStruct((peers, SPAN_MAX * steps, cols), jnp.float32),
        ),
        in_specs=[vmem, hbm, hbm],
        out_specs=(vmem, vmem),
        scratch_shapes=[
            pltpu.VMEM(trans_logits.shape, jnp.float32),
            pltpu.VMEM(emit_logits.shape, jnp.float32),
            dma((2,)),
            pltpu.VMEM((SPAN_MAX, steps, 128), jnp.int32),
            dma((SPAN_MAX,)), dma((SPAN_MAX,)),
            dma((2 * peers,)), dma((block_rows,)),
            dma((peers,)), dma((peers,)),
        ],
        compiler_params=pltpu.CompilerParams(
            collective_id=0, has_side_effects=True, vmem_limit_bytes=32 * 2**20),
        name="gather",
    )(obs_wide, trans_logits, emit_logits)

    high, low, gain = pl.pallas_call(
        functools.partial(form_kernel, groups),
        out_shape=(
            jax.ShapeDtypeStruct((block_rows, block, cols), jnp.bfloat16),
            jax.ShapeDtypeStruct((block_rows, block, cols), jnp.bfloat16),
            jax.ShapeDtypeStruct((1, cols), jnp.float32),
        ),
        in_specs=[hbm, vmem, vmem],
        out_specs=(vmem, vmem, vmem),
        scratch_shapes=[
            pltpu.SMEM((filled, block_rows), jnp.int32),
            dma,
            pltpu.VMEM((block_rows, block, cols), jnp.float32),
            pltpu.VMEM((block_rows, block, cols), jnp.bfloat16),
            pltpu.VMEM((block_rows, block, block), jnp.float32),
        ],
        compiler_params=pltpu.CompilerParams(vmem_limit_bytes=40 * 2**20),
        name="form",
    )(band_cols.T, blocks, emis)

    return pl.pallas_call(
        functools.partial(chain_kernel, groups, peers),
        out_shape=jax.ShapeDtypeStruct((1, cols), jnp.float32),
        in_specs=[vmem] * 4,
        out_specs=vmem,
        scratch_shapes=[
            pltpu.VMEM((peers, 1, cols), jnp.float32),
            pltpu.VMEM((peers, 1, cols), jnp.float32),
            pltpu.VMEM((1, cols), jnp.float32),
            dma((peers,)), dma((SPAN_MAX + 1, peers)),
            dma((peers,)), dma((peers,)), dma,
            pltpu.SemaphoreType.REGULAR,
        ],
        compiler_params=pltpu.CompilerParams(
            collective_id=1, has_side_effects=True, vmem_limit_bytes=32 * 2**20),
        name="chain",
    )(init_logits.reshape(peers, 1, cols), high, low, gain)


def solution(mesh):
    return jax.shard_map(
        on_device,
        mesh=mesh,
        in_specs=(P("tm"), P(None, "state"), P("state", None, None, None), P(), P()),
        out_specs=P("tm", "state"),
        check_vma=False,
    )
```

```python
import functools
import math

import jax
import jax.numpy as jnp
from jax import lax
from jax.experimental import pallas as pl
from jax.experimental.pallas import tpu as pltpu
from jax.sharding import PartitionSpec as P

SMOOTH = 0.001
MESH = pl.DeviceIdType.MESH
DEEP = 16
RISES = (5, 9, 17, 29, 33, 45)
SPAN_MAX = 1 + len(RISES)


def span_of(group):
    span = jnp.int32(1)
    for rise in RISES:
        span = span + (group >= rise).astype(jnp.int32)
    return span


def group_at(place, groups):
    high = groups // DEEP
    y, z = place // DEEP, place % DEEP
    return jnp.where(z < high, y * high + z, z * high + y)


def place_of(group, groups):
    high = groups // DEEP
    return jnp.where(
        group < high * high, group // high * DEEP + group % high, group % high * DEEP + group // high)


def when_all(*conditions):
    return pl.when(functools.reduce(jnp.logical_and, conditions))


def inverse_of(value):
    def halves(x):
        scaled = x * 4097.0
        high = scaled - (scaled - x)
        return high, x - high

    quotient = 1.0 / value
    product = value * quotient
    value_high, value_low = halves(value)
    quotient_high, quotient_low = halves(quotient)
    excess = value_high * quotient_high - product
    excess = excess + value_high * quotient_low + value_low * quotient_high + value_low * quotient_low
    return quotient + quotient * ((1.0 - product) - excess)


def gather_kernel(groups, peers, obs_ref, trans_ref, emit_ref, blocks_ref, emis_ref, obs_all, obs_send, obs_recv, blk_send, blk_recv, em_send, em_recv):
    place = lax.axis_index("tm")
    group = group_at(place, groups)
    me = lax.axis_index("state")
    core = me % 2
    chip = me // 2
    chips = peers // 2
    sibling = me + 1 - 2 * core
    own_rows = trans_ref.shape[0]
    steps = obs_all.shape[1]

    def feeds(back):
        later = place + back
        used = jnp.logical_and(later < groups, span_of(later) > back)
        target = place_of(later, groups)
        return used, target, target == place

    def fed_by(back):
        used = jnp.logical_and(group >= back, span_of(group) > back)
        origin = group - back
        return used, origin, origin == place

    barrier = pltpu.get_barrier_semaphore()
    for other in range(1, peers):
        pl.semaphore_signal(barrier, inc=1, device_id=(place, (me + other) % peers), device_id_type=MESH)
    expected = jnp.int32(peers - 1)
    for back in range(SPAN_MAX):
        for side in (feeds, fed_by):
            used, partner, same = side(back)
            far = jnp.logical_and(used, jnp.logical_not(same))

            @pl.when(far)
            def _():
                pl.semaphore_signal(barrier, inc=1, device_id=(partner, me), device_id_type=MESH)

            expected = expected + far.astype(jnp.int32)

    for row in range(own_rows):
        tiles = [trans_ref[row, k] for k in range(trans_ref.shape[1])]
        top = jnp.max(functools.reduce(jnp.maximum, tiles), axis=1, keepdims=True)
        tiles = [jnp.exp(tile - top) for tile in tiles]
        width = tiles[0].shape[1]
        totals = []
        for tile in tiles:
            for shift in (16, 32, 64, 8, 4, 2, 1):
                tile = tile + pltpu.roll(tile, width - shift, 1)
            totals.append(tile)
        inverse = inverse_of(functools.reduce(jnp.add, totals)[:, :1])
        for k, tile in enumerate(tiles):
            blocks_ref[own_rows * me + row, :, k * width:(k + 1) * width] = (
                (1.0 - SMOOTH) * (tile * inverse)).astype(jnp.bfloat16)

    pl.semaphore_wait(barrier, expected)

    def obs_copy(back, target):
        return pltpu.make_async_remote_copy(
            src_ref=obs_ref, dst_ref=obs_all.at[back], send_sem=obs_send.at[back], recv_sem=obs_recv.at[back],
            device_id=(target, me), device_id_type=MESH)

    def block_copy(owner, row, target, sem):
        part = blocks_ref.at[own_rows * owner + row]
        return pltpu.make_async_remote_copy(
            src_ref=part, dst_ref=part, send_sem=blk_send.at[sem], recv_sem=blk_recv.at[own_rows * owner + row],
            device_id=(place, target), device_id_type=MESH)

    def emis_copy(owner, target, sem):
        part = emis_ref.at[owner]
        return pltpu.make_async_remote_copy(
            src_ref=part, dst_ref=part, send_sem=em_send.at[sem], recv_sem=em_recv.at[owner],
            device_id=(place, target), device_id_type=MESH)

    for back in range(SPAN_MAX):
        used, target, same = feeds(back)

        @when_all(used, jnp.logical_not(same))
        def _():
            obs_copy(back, target).start()

        @when_all(used, same)
        def _():
            obs_all[back] = obs_ref[...]

        @pl.when(jnp.logical_not(fed_by(back)[0]))
        def _():
            obs_all[back] = jnp.zeros(obs_ref.shape, obs_ref.dtype)

    sent = []

    def send_block(owner, row, target):
        sent.append(block_copy(owner, row, target, len(sent)))
        sent[-1].start()

    right = 2 * ((chip + 1) % chips) + core
    left = 2 * ((chip + chips - 1) % chips) + core
    across = 2 * ((chip + 2) % chips) + core
    for row, target in ((0, right), (1, left), (1, right), (0, left), (0, sibling), (1, sibling)):
        send_block(me, row, target)

    logits = emit_ref[...]
    weights = jnp.exp(logits - jnp.max(logits, axis=0, keepdims=True))
    table = weights / jnp.sum(weights, axis=0, keepdims=True)
    for back in range(SPAN_MAX):
        used, origin, same = fed_by(back)

        @when_all(used, jnp.logical_not(same))
        def _():
            obs_copy(back, origin).wait_recv()

    symbols = logits.shape[0]
    seen = obs_all[...].reshape(SPAN_MAX * steps, obs_all.shape[2])
    lane = lax.broadcasted_iota(jnp.int32, seen.shape, 1)
    onehot = jnp.concatenate(
        [(seen == lane + first).astype(jnp.float32) for first in range(0, symbols, seen.shape[1])], axis=1)
    emis_ref[me] = jnp.dot(onehot, table, precision=lax.Precision.HIGHEST, preferred_element_type=jnp.float32)
    for other in range(1, peers):
        emis_copy(me, (me + other) % peers, other).start()

    for owner, row, onward in ((left, 0, right), (right, 1, left), (left, 1, None), (right, 0, None),
                               (across, 0, None), (across, 1, None)):
        block_copy(owner, row, sibling, 0).wait_recv()
        if onward is not None:
            send_block(owner, row, onward)
        send_block(owner, row, sibling)
    for away in range(chips):
        for row in range(own_rows):
            block_copy(2 * ((chip + away) % chips) + 1 - core, row, sibling, 0).wait_recv()
    for other in range(1, peers):
        emis_copy((me + other) % peers, sibling, 0).wait_recv()
    for copy in sent:
        copy.wait_send()
    for other in range(1, peers):
        emis_copy(me, (me + other) % peers, other).wait_send()
    for back in range(SPAN_MAX):
        used, target, same = feeds(back)

        @when_all(used, jnp.logical_not(same))
        def _():
            obs_copy(back, target).wait_send()


def form_kernel(groups, band_hbm, blocks_ref, emis_ref, result_ref, gain_ref, band_here, loaded, matrix, scaled, columns):
    group = group_at(lax.axis_index("tm"), groups)
    me = lax.axis_index("state")
    block_rows, block, cols = matrix.shape
    filled = blocks_ref.shape[2] // block
    states = block_rows * block
    log_symbols = math.log(256.0)
    steps = 8
    row_id = lax.broadcasted_iota(jnp.int32, (block, cols), 0)
    col_id = lax.broadcasted_iota(jnp.int32, (block, cols), 1)
    load = pltpu.make_async_copy(band_hbm, band_here, loaded)
    load.start()
    for r in range(block_rows):
        matrix[r] = (row_id + r * block == col_id + me * cols).astype(jnp.float32)

    def row_at(index, owner):
        tile = pl.ds(pl.multiple_of((index // steps) * steps, steps), steps)
        now = lax.broadcasted_iota(jnp.int32, (steps, cols), 0) == steps - 1 - index % steps
        return jnp.sum(jnp.where(now, emis_ref[owner, tile, :], 0.0), axis=0, keepdims=True)

    def set_column(r, row):
        start = r * block % cols
        columns[r] = jnp.broadcast_to(row[:, start:start + block], (block, block)).T

    for r in range(block_rows):
        set_column(r, row_at(0, r * block // cols))
    load.wait()

    def step(index, carry):
        inverse, log_scale = carry
        col_sum = jnp.zeros((8, cols), jnp.float32)
        for r in range(block_rows):
            column = jnp.concatenate([columns[r]] * (cols // block), axis=1)
            part = column * (matrix[r] * inverse)
            scaled[r] = part.astype(jnp.bfloat16)
            col_sum = col_sum + jnp.sum(part.reshape(block // 8, 8, cols), axis=0)
        smooth = (SMOOTH / states) * jnp.sum(col_sum, axis=0, keepdims=True)
        peak = jnp.zeros((8, cols), jnp.float32)
        following = jnp.minimum(index + 1, emis_ref.shape[1] - 1)
        for r in range(block_rows):
            picked = jnp.concatenate([scaled[band_here[k, r]] for k in range(filled)], axis=0)
            product = jnp.dot(blocks_ref[r], picked, preferred_element_type=jnp.float32) + smooth
            matrix[r] = product
            if r * block % cols == 0:
                row = row_at(following, r * block // cols)
            set_column(r, row)
            peak = jnp.maximum(peak, jnp.max(product.reshape(block // 8, 8, cols), axis=0))
        peak = jnp.max(peak, axis=0, keepdims=True)
        return 1.0 / peak, log_scale + (jnp.log(peak) + log_symbols)

    inverse, log_scale = lax.fori_loop(
        0, steps * span_of(group), step, (jnp.ones((1, cols), jnp.float32), jnp.zeros((1, cols), jnp.float32)))
    gain_ref[...] = jnp.exp(log_scale)
    for r in range(block_rows):
        result_ref[r] = (matrix[r] * inverse).astype(jnp.bfloat16)


def chain_kernel(groups, peers, init_ref, matrix_ref, gain_ref, out_ref,
                 parts, owned, mine, recv, send, own_send, own_recv, own_local, ready):
    place = lax.axis_index("tm")
    group = group_at(place, groups)
    me = lax.axis_index("state")
    source = group - span_of(group)
    has_source = source >= 0
    feeds = [
        jnp.logical_and(group + ahead < groups, span_of(group + ahead) == ahead)
        for ahead in range(1, SPAN_MAX + 1)
    ]
    origin = place_of(place, groups)
    at_home = group == place
    owned_later = place > group
    owned_earlier = place < group
    owner_first = group_at(group, groups) < group
    owner_later = group_at(group, groups) > group

    barrier = pltpu.get_barrier_semaphore()
    expected = jnp.int32(0)

    def greet(condition, target):
        @pl.when(condition)
        def _():
            for peer in range(peers):
                pl.semaphore_signal(barrier, inc=1, device_id=(target, peer), device_id_type=MESH)

    @pl.when(at_home)
    def _():
        for other in range(1, peers):
            pl.semaphore_signal(barrier, inc=1, device_id=(place, (me + other) % peers), device_id_type=MESH)

    greet(has_source, place_of(source, groups))
    expected = expected + (peers - 1) * at_home.astype(jnp.int32) + peers * has_source.astype(jnp.int32)
    for ahead, fed in enumerate(feeds, 1):
        greet(fed, place_of(group + ahead, groups))
        expected = expected + peers * fed.astype(jnp.int32)
    greet(owned_later, origin)
    greet(owner_later, group)
    expected = expected + peers * (owned_earlier.astype(jnp.int32) + owner_first.astype(jnp.int32))

    def onward(ahead, slot, peer):
        return pltpu.make_async_remote_copy(
            src_ref=mine, dst_ref=parts.at[slot], send_sem=send.at[ahead, peer], recv_sem=recv.at[slot],
            device_id=(place_of(group + ahead, groups), peer), device_id_type=MESH)

    def to_owner(slot, peer):
        return pltpu.make_async_remote_copy(
            src_ref=mine, dst_ref=owned.at[slot], send_sem=own_send.at[peer], recv_sem=own_recv.at[slot],
            device_id=(group, peer), device_id_type=MESH)

    pl.semaphore_wait(barrier, expected)

    @pl.when(owned_earlier)
    def _():
        for peer in range(peers):
            pl.semaphore_signal(ready, inc=1, device_id=(origin, peer), device_id_type=MESH)

    @pl.when(jnp.logical_not(has_source))
    def _():
        parts[...] = jnp.exp(init_ref[...] - jnp.max(init_ref[...]))

    @pl.when(has_source)
    def _():
        for peer in range(peers):
            onward(0, peer, 0).wait_recv()

    width = parts.shape[2]
    first_row = lax.broadcasted_iota(jnp.int32, (16, width), 0) == 0
    mixed = jnp.zeros((16, width), jnp.float32)
    total = jnp.zeros((1, width), jnp.float32)
    depth = matrix_ref.shape[1]
    for peer in range(peers):
        part = parts[peer]
        total = total + part
        spread = jnp.broadcast_to(part, (16, width))
        rest = spread - spread.astype(jnp.bfloat16).astype(jnp.float32)
        both = jnp.where(first_row, spread, rest).astype(jnp.bfloat16)
        rows = slice(peer * (width // depth), (peer + 1) * (width // depth))
        mixed += jnp.dot(both, matrix_ref[rows].reshape(width, width), preferred_element_type=jnp.float32)
    norm = gain_ref[...] / jnp.sum(total, axis=1, keepdims=True)
    mine[...] = (mixed[0:1] + mixed[1:2]) * norm

    for ahead, fed in enumerate(feeds, 1):
        @pl.when(fed)
        def _():
            for turn in (4, 5, 2, 3, 6, 7, 1, 0):
                onward(ahead, me, (me - me % 2 + turn) % peers).start()

    @pl.when(owner_later)
    def _():
        pl.semaphore_wait(ready, peers)

    @pl.when(at_home)
    def _():
        pltpu.make_async_copy(mine, owned.at[me], own_local).start()
        for other in range(1, peers):
            to_owner(me, (me + other) % peers).start()
        pltpu.make_async_copy(mine, owned.at[me], own_local).wait()
        for other in range(1, peers):
            to_owner((me + other) % peers, 0).wait_recv()
        for other in range(1, peers):
            to_owner(me, (me + other) % peers).wait_send()

    @pl.when(jnp.logical_not(at_home))
    def _():
        for peer in range(peers):
            to_owner(me, peer).start()
        for slot in range(peers):
            to_owner(slot, 0).wait_recv()
        for peer in range(peers):
            to_owner(me, peer).wait_send()

    whole = jnp.zeros((1, width), jnp.float32)
    for slot in range(peers):
        whole = whole + owned[slot]
    out_ref[...] = jnp.log(owned[me]) - jnp.log(jnp.sum(whole, axis=1, keepdims=True))
    for ahead, fed in enumerate(feeds, 1):
        @pl.when(fed)
        def _():
            for peer in range(peers):
                onward(ahead, me, peer).wait_send()


def on_device(obs, emit_logits, trans_logits, band_cols, init_logits):
    peers = lax.axis_size("state")
    groups = lax.axis_size("tm")
    cols = emit_logits.shape[1]
    own_rows, filled, block, _ = trans_logits.shape
    block_rows = own_rows * peers
    steps = obs.shape[0]
    vmem = pl.BlockSpec(memory_space=pltpu.VMEM)
    dma = pltpu.SemaphoreType.DMA

    hbm = pl.BlockSpec(memory_space=pltpu.HBM)
    obs_wide = jnp.broadcast_to(obs[:, None], (steps, 128))
    blocks, emis = pl.pallas_call(
        functools.partial(gather_kernel, groups, peers),
        out_shape=(
            jax.ShapeDtypeStruct((block_rows, block, filled * block), jnp.bfloat16),
            jax.ShapeDtypeStruct((peers, SPAN_MAX * steps, cols), jnp.float32),
        ),
        in_specs=[vmem] * 3,
        out_specs=(vmem, vmem),
        scratch_shapes=[
            pltpu.VMEM((SPAN_MAX, steps, 128), jnp.int32),
            dma((SPAN_MAX,)), dma((SPAN_MAX,)),
            dma((2 * peers,)), dma((block_rows,)),
            dma((peers,)), dma((peers,)),
        ],
        compiler_params=pltpu.CompilerParams(
            collective_id=0, has_side_effects=True, vmem_limit_bytes=32 * 2**20),
        name="gather",
    )(obs_wide, trans_logits, emit_logits)

    matrix, gain = pl.pallas_call(
        functools.partial(form_kernel, groups),
        out_shape=(
            jax.ShapeDtypeStruct((block_rows, block, cols), jnp.bfloat16),
            jax.ShapeDtypeStruct((1, cols), jnp.float32),
        ),
        in_specs=[hbm, vmem, vmem],
        out_specs=(vmem, vmem),
        scratch_shapes=[
            pltpu.SMEM((filled, block_rows), jnp.int32),
            dma,
            pltpu.VMEM((block_rows, block, cols), jnp.float32),
            pltpu.VMEM((block_rows, block, cols), jnp.bfloat16),
            pltpu.VMEM((block_rows, block, block), jnp.float32),
        ],
        compiler_params=pltpu.CompilerParams(vmem_limit_bytes=40 * 2**20),
        name="form",
    )(band_cols.T, blocks, emis)

    return pl.pallas_call(
        functools.partial(chain_kernel, groups, peers),
        out_shape=jax.ShapeDtypeStruct((1, cols), jnp.float32),
        in_specs=[vmem] * 3,
        out_specs=vmem,
        scratch_shapes=[
            pltpu.VMEM((peers, 1, cols), jnp.float32),
            pltpu.VMEM((peers, 1, cols), jnp.float32),
            pltpu.VMEM((1, cols), jnp.float32),
            dma((peers,)), dma((SPAN_MAX + 1, peers)),
            dma((peers,)), dma((peers,)), dma,
            pltpu.SemaphoreType.REGULAR,
        ],
        compiler_params=pltpu.CompilerParams(
            collective_id=1, has_side_effects=True, vmem_limit_bytes=32 * 2**20),
        name="chain",
    )(init_logits.reshape(peers, 1, cols), matrix, gain)


def solution(mesh):
    return jax.shard_map(
        on_device,
        mesh=mesh,
        in_specs=(P("tm"), P(None, "state"), P("state", None, None, None), P(), P()),
        out_specs=P("tm", "state"),
        check_vma=False,
    )
```
